32 devices in a mesh: groups: 2 (over x), fsdp: 16 (over z, y, core).
Axes of the slice: x: 2, y: 2, z: 4, core: 2. Of those that a mesh axis runs over, the one named last changes fastest.
Arguments:
- obs_feat: bfloat16 [12288, 2048], P(('groups', 'fsdp')), parts along dimension 0, may hold values from -6 to 6
- reward: float32 [512, 24], P(('groups', 'fsdp')), parts along dimension 0, may hold values from -22 to 22
- value_old: float32 [512, 25], P(('groups', 'fsdp')), parts along dimension 0, may hold values from -6 to 6
- done: int32 [512, 24], P(('groups', 'fsdp')), parts along dimension 0, may hold values 0 or 1
- minibatch_perm: int32 [12288], P(('groups', 'fsdp')), parts along dimension 0, may hold values from 0 to 6143, as said below
- old_mean: bfloat16 [12288, 12], P(('groups', 'fsdp')), parts along dimension 0, may hold values from -6 to 6
- noise: bfloat16 [12288, 12], P(('groups', 'fsdp')), parts along dimension 0, may hold values from -6 to 6
- gain_in: float32 [2048], replicated, may hold values from 0.5 to 1.5
- out_weight: bfloat16 [2048, 2048], P('fsdp'), may hold values from -0.125 to 0.125
- head_weight: bfloat16 [2048, 13], replicated, may hold values from -0.125 to 0.125
- log_std: float32 [12], replicated, may hold values from 0.7 to 1.3
Outputs:
- hidden_out: bfloat16 [12288, 2048], P(('groups', 'fsdp')), parts along dimension 0
- grad_weight: float32 [4096, 2048], P(('groups', 'fsdp')), parts along dimension 0
- grad_head: float32 [4096, 13], P('groups'), parts along dimension 0
- grad_std: float32 [24], P('groups'), parts along dimension 0
The draws below stay inside these ranges and needn't reach their ends.
There are 2 independent parts, one for each index of `groups`. The reference program is written for one: setup_inputs(seed, part) draws one part's arguments, and reference() takes and returns one part's arrays. A program takes and returns all parts, laid end to end along the dimension named above; an argument that names none is the same for every part. Nothing has to cross between parts.
Inputs may be any that keep to these rules, and one draw needn't show every extreme that they name: `minibatch_perm`: rows of one index of fsdp go 24 to each index of fsdp; the block of 384 minibatch positions of index j holds at positions j * 384 + s * 24 + c the rows from index s; a permutation of all rows.
All inputs are finite; a program needn't handle non-finite values. No bound on the sum of `done` on one device may be relied on, other than what follows from the above.
Results may differ from the reference program's by a relative error of at most 0.0095.
Values may be sent and summed in bfloat16 or wider, within the bound.
A program may use at most 128 MiB of HBM per device.

```python
import jax
import jax.numpy as jnp
from jax import lax

D = 2048
ACT = 12
STEPS = 24
ENVS = 256
ROWS_DEV = 384
ROWS = 6144
PEER = 24
N_FSDP = 16


def draw_reward(key, part):
    first = jax.random.fold_in(jax.random.fold_in(key, 11), 0)
    env_pos = jnp.arange(ENVS, dtype=jnp.float32) / ENVS
    rising = jnp.exp(jnp.log(3.0) * env_pos)[:, None]
    values = jnp.clip(jax.random.normal(first, (ENVS, STEPS), jnp.float32), -5.0, 5.0) * rising
    return jnp.clip(values, -22.0, 22.0).astype(jnp.float32)


def draw_minibatch_perm(key, part):
    keys = jax.random.split(jax.random.fold_in(key, 23), N_FSDP)
    shuffled = jax.vmap(lambda single: jax.random.permutation(single, ROWS_DEV))(keys).astype(jnp.int32)
    source = jnp.arange(N_FSDP, dtype=jnp.int32)[:, None]
    target = shuffled // PEER
    within = shuffled % PEER
    return (target * ROWS_DEV + source * PEER + within).reshape(-1).astype(jnp.int32)


def place_ends(result, own_key, low, high):
    spot = [jax.random.randint(jax.random.fold_in(own_key, axis), (), 0, length) for axis, length in enumerate(result.shape)]
    longest = result.shape.index(max(result.shape))
    neighbour = spot[:longest] + [(spot[longest] + 1) % result.shape[longest]] + spot[longest + 1:]
    return result.at[tuple(spot)].set(low).at[tuple(neighbour)].set(high)


def level_of(key, shape, cuts, low, top_value):
    def one(dim, parts):
        steps = jax.random.uniform(jax.random.fold_in(jax.random.fold_in(key, 6), dim), (parts,), jnp.float32, low / len(cuts), top_value / len(cuts))
        return jnp.repeat(jnp.exp(steps), shape[dim] // parts).reshape((-1,) + (1,) * (len(shape) - dim - 1))

    loudness = one(*cuts[0])
    for cut in cuts[1:]:
        loudness = loudness * one(*cut)
    return loudness


def gaussian(stream_key, dims, deviation, limit, shards=(), kind=jnp.bfloat16):
    array = jax.random.normal(stream_key, dims, jnp.float32) * deviation
    if len(shards) > 0:
        array = level_of(stream_key, dims, shards, -0.22, 0.18) * array
    return jnp.clip(array, min=-limit, max=limit).astype(kind)


def setup_inputs(seed: int = 0, part: int = 0) -> dict:
    seeds = jax.random.split(jax.random.key(seed), 12)
    own_keys = jax.random.split(jax.random.fold_in(seeds[11], part), 12)
    return {
        "obs_feat": gaussian(own_keys[0], (ROWS, D), 1.0, 6.0, ((0, 16),)),
        "reward": draw_reward(jax.random.fold_in(jax.random.fold_in(seeds[11], part), 71), part),
        "value_old": gaussian(own_keys[2], (ENVS, STEPS + 1), 1.0, 6.0, ((0, 16),), jnp.float32),
        "done": place_ends((jax.random.randint(own_keys[3], (ENVS, STEPS), 0, 32) < 1).astype(jnp.int32), jax.random.fold_in(own_keys[3], 1), 0, 1),
        "minibatch_perm": draw_minibatch_perm(jax.random.fold_in(jax.random.fold_in(seeds[11], part), 71), part),
        "old_mean": gaussian(own_keys[5], (ROWS, ACT), 1.0, 6.0, ((0, 16),)),
        "noise": gaussian(own_keys[6], (ROWS, ACT), 1.0, 6.0, ((0, 16),)),
        "gain_in": jnp.clip(1.0 + 0.1 * jax.random.normal(seeds[7], (D,), jnp.float32), 0.5, 1.5),
        "out_weight": gaussian(seeds[8], (D, D), D ** -0.5, 0.125, ((0, 16),)),
        "head_weight": gaussian(seeds[9], (D, ACT + 1), D ** -0.5, 0.125),
        "log_std": jnp.clip(jax.random.uniform(seeds[10], (ACT,), jnp.float32, 0.7, 1.3), 0.7, 1.3),
    }


GAMMA = 0.99
LAMBDA_GAE = 0.95
CLIP_EPS = 0.2
NORM_EPS = 1e-05

def advantages(reward, value_old, done):
    keep = 1.0 - done.astype(jnp.float32)
    deltas = reward + GAMMA * value_old[:, 1:] * keep - value_old[:, :-1]

    def walk(carry, inputs):
        dstep, kstep = inputs
        carry = dstep + GAMMA * LAMBDA_GAE * kstep * carry
        return (carry, carry)
    start = jnp.zeros((reward.shape[0],), jnp.float32)
    _, stacked = lax.scan(walk, start, (deltas.T, keep.T), reverse=True)
    gae = stacked.T
    return (gae.reshape(-1), (gae + value_old[:, :-1]).reshape(-1))

def row_block(rows_x, old_mean, noise, adv_b, ret_b, gain_in, out_weight, head_weight, log_std, scale):
    xf = rows_x.astype(jnp.float32)
    normed = (xf * lax.rsqrt(lax.optimization_barrier(jnp.mean(xf * xf, -1, keepdims=True)) + NORM_EPS) * gain_in).astype(jnp.bfloat16)
    hidden = xf + jnp.dot(normed, out_weight, preferred_element_type=jnp.float32)
    rinv = lax.rsqrt(lax.optimization_barrier(jnp.mean(hidden * hidden, -1, keepdims=True)) + NORM_EPS)
    hnorm = hidden * rinv
    hnorm_b = hnorm.astype(jnp.bfloat16)
    heads = jnp.dot(hnorm_b, head_weight, preferred_element_type=jnp.float32)
    nact = log_std.shape[0]
    mean_act = heads[:, :nact]
    value = heads[:, nact]
    std_dev = jnp.exp(log_std)
    offset = old_mean.astype(jnp.float32) - mean_act
    sample = noise.astype(jnp.float32)
    logr = lax.optimization_barrier(jnp.sum(-sample * offset / std_dev - offset * offset / (2.0 * std_dev * std_dev), -1))
    ratio = jnp.exp(logr)
    advant = adv_b.astype(jnp.float32)
    clipped = jnp.clip(ratio, 1.0 - CLIP_EPS, 1.0 + CLIP_EPS)
    active = ratio * advant <= clipped * advant
    gratio = jnp.where(active, -scale * advant, 0.0)
    glogr = gratio * ratio
    gmean = glogr[:, None] * (sample / std_dev + offset / (std_dev * std_dev))
    gvalue = scale * (value - ret_b.astype(jnp.float32))
    std_part = lax.optimization_barrier(jnp.sum(glogr[:, None] * (sample * offset / std_dev + offset * offset / (std_dev * std_dev)), 0))
    ghead = jnp.concatenate([gmean, gvalue[:, None]], 1)
    head_part = jnp.dot(hnorm_b.astype(jnp.float32).T, ghead, precision=lax.Precision.HIGHEST)
    ghn = jnp.dot(ghead, head_weight.astype(jnp.float32).T, precision=lax.Precision.HIGHEST)
    ghid = rinv * (ghn - hnorm * lax.optimization_barrier(jnp.mean(ghn * hnorm, -1, keepdims=True)))
    ghid_b = ghid.astype(jnp.bfloat16)
    return (hidden.astype(jnp.bfloat16), normed, ghid_b, head_part, std_part)

def reference(obs_feat, reward, value_old, done, minibatch_perm, old_mean, noise, gain_in, out_weight, head_weight, log_std):
    gae, returns = advantages(reward, value_old, done)
    mean_adv = jnp.sum(gae) / ROWS
    var_adv = jnp.sum(gae * gae) / ROWS - mean_adv * mean_adv
    adv_b = ((gae - mean_adv) * lax.rsqrt(var_adv + NORM_EPS)).astype(jnp.bfloat16)
    ret_b = returns.astype(jnp.bfloat16)
    scale = 1.0 / jnp.sqrt(jnp.float32(ROWS))
    nblock = ROWS // ROWS_DEV

    def one_block(carry, inputs):
        wsum, hsum, ssum = carry
        bx, bm, bn, ba, br = inputs
        hid_b, normed, ghid_b, head_part, std_part = row_block(bx, bm, bn, ba, br, gain_in, out_weight, head_weight, log_std, scale)
        wpart = lax.dot_general(normed, ghid_b, (((0,), (0,)), ((), ())), preferred_element_type=jnp.float32)
        return ((wsum + wpart, hsum + head_part, ssum + std_part), hid_b)
    init = (jnp.zeros((D, D), jnp.float32), jnp.zeros((D, ACT + 1), jnp.float32), jnp.zeros((ACT,), jnp.float32))
    inputs = (obs_feat.reshape(nblock, ROWS_DEV, D), old_mean.reshape(nblock, ROWS_DEV, ACT), noise.reshape(nblock, ROWS_DEV, ACT), adv_b.reshape(nblock, ROWS_DEV), ret_b.reshape(nblock, ROWS_DEV))
    (grad_weight, grad_head, grad_std), hid_all = lax.scan(one_block, init, inputs)
    hidden_out = jnp.zeros((ROWS, D), jnp.bfloat16).at[minibatch_perm].set(hid_all.reshape(ROWS, D))
    return (hidden_out, grad_weight, grad_head, grad_std)
```

```python
import functools

import jax
import jax.numpy as jnp
from jax import lax
from jax.experimental import pallas as pl
from jax.experimental.pallas import tpu as pltpu
from jax.sharding import PartitionSpec as P

GAMMA = 0.99
LAMBDA_GAE = 0.95
CLIP_EPS = 0.2
NORM_EPS = 1e-05
MESH = pl.DeviceIdType.MESH
TILE = 512


def chip_at(pos, ring):
    half = ring // 2
    col = pos // half
    row = col * (ring - 1 - pos) + (1 - col) * pos
    return 2 * row + col


class Ring:
    def __init__(self, n):
        self.n = n
        self.me = lax.axis_index("fsdp")
        self.ring = n // 2
        self.core = lax.rem(self.me, 2)
        chip = self.me // 2
        col = lax.rem(chip, 2)
        row = chip // 2
        self.pos = col * (self.ring - 1 - row) + (1 - col) * row
        self.step = 1 - 2 * self.core
        self.sibling = self.me + self.step

    def device(self, ahead, core):
        pos = lax.rem(self.pos + ahead + self.ring, self.ring)
        return 2 * chip_at(pos, self.ring) + core

    def down(self):
        return self.device(self.step, self.core)


def enter(n, me):
    barrier = pltpu.get_barrier_semaphore()

    @pl.loop(1, n)
    def _(k):
        pl.semaphore_signal(
            barrier, inc=1, device_id={"fsdp": lax.rem(me + k, n)}, device_id_type=MESH
        )

    pl.semaphore_wait(barrier, n - 1)


def remote(src, dst, send, recv, device):
    return pltpu.make_async_remote_copy(
        src_ref=src,
        dst_ref=dst,
        send_sem=send,
        recv_sem=recv,
        device_id={"fsdp": device},
        device_id_type=MESH,
    )


def pieces(rows):
    count = 2 if rows % 32 == 0 else 1
    return [pl.ds(i * (rows // count), rows // count) for i in range(count)]


def spread(n, me, source_of, dst, send, recv):
    @pl.loop(1, n)
    def _(k):
        peer = lax.rem(me + k, n)
        remote(source_of(peer), dst.at[me], send, recv, peer).start()


def collect(n, slots, sem):
    part = slots.at[pl.ds(0, n - 1)]
    pltpu.make_async_copy(part, part, sem).wait()


def forward_kernel(
    n, x_ref, normed_ref, stat_ref, w_ref, hidden_ref, sums_ref,
    held, stats, local_sem, ring_send, ring_recv, sib_send, sib_recv, stat_send, stat_recv,
):
    r = Ring(n)
    me, last = r.me, r.ring - 1
    own = pltpu.make_async_copy(w_ref, held.at[me], local_sem)
    own.start()
    enter(n, me)
    cuts = pieces(held.shape[1])
    down = r.down()

    def ring_copy(owner, step, i):
        part = held.at[owner, cuts[i]]
        return remote(part, part, ring_send.at[step, i], ring_recv.at[step, i], down)

    def sib_copy(owner, step, i):
        part = held.at[owner, cuts[i]]
        return remote(part, part, sib_send.at[step, i], sib_recv.at[step, i], r.sibling)

    def mine(step):
        return r.device(-r.step * step, r.core)

    def theirs(step):
        return r.device(r.step * step, 1 - r.core)

    def add(owner):
        for j in range(0, hidden_ref.shape[1], TILE):
            cols = pl.ds(j, TILE)
            hidden_ref[:, cols] += jnp.dot(
                normed_ref[owner], held[owner, :, cols], preferred_element_type=jnp.float32
            )

    own.wait()
    for i in range(len(cuts)):
        ring_copy(me, 1, i).start()
        sib_copy(me, 0, i).start()
    spread(n, me, lambda peer: stat_ref, stats, stat_send, stat_recv)
    stats[me] = stat_ref[...]
    hidden_ref[...] = x_ref[...].astype(jnp.float32)

    def hop(step, _):
        owner = mine(step)
        for i in range(len(cuts)):
            ring_copy(owner, step, i).wait_recv()

            @pl.when(step < last)
            def _():
                ring_copy(owner, step + 1, i).start()

            sib_copy(owner, step, i).start()
            if i == 0:
                add(mine(step - 1))
        for i in range(len(cuts)):
            sib_copy(theirs(step - 1), step - 1, i).wait_recv()
        add(theirs(step - 1))
        return 0

    lax.fori_loop(1, r.ring, hop, 0)
    add(mine(last))
    for i in range(len(cuts)):
        sib_copy(theirs(last), last, i).wait_recv()
    add(theirs(last))
    collect(n, stats, stat_recv)
    sums_ref[...] = jnp.sum(stats[...], 0)
    collect(n, stats, stat_send)

    def drain(step, _):
        owner = mine(step)
        for i in range(len(cuts)):
            @pl.when(step < last)
            def _():
                ring_copy(owner, step + 1, i).wait_send()

            sib_copy(owner, step, i).wait_send()
        return 0

    lax.fori_loop(0, r.ring, drain, 0)


def forward(n, x, normed, stat, weight):
    rows, width = x.shape
    shard = weight.shape[0]
    blocks = normed.reshape(rows, n, shard).transpose(1, 0, 2)
    count = len(pieces(shard))
    vmem = pl.BlockSpec(memory_space=pltpu.VMEM)
    sems = pltpu.SemaphoreType.DMA
    return pl.pallas_call(
        functools.partial(forward_kernel, n),
        name="forward",
        out_shape=(
            jax.ShapeDtypeStruct((rows, width), jnp.float32),
            jax.ShapeDtypeStruct(stat.shape, jnp.float32),
        ),
        in_specs=[vmem, vmem, vmem, pl.BlockSpec(memory_space=pl.ANY)],
        out_specs=(vmem, vmem),
        scratch_shapes=[
            pltpu.VMEM((n, shard, width), jnp.bfloat16),
            pltpu.VMEM((n,) + stat.shape, jnp.float32),
            sems(()),
            sems((n // 2, count)),
            sems((n // 2, count)),
            sems((n // 2, count)),
            sems((n // 2, count)),
            sems(()),
            sems(()),
        ],
        compiler_params=pltpu.CompilerParams(
            collective_id=0, has_side_effects=True, vmem_limit_bytes=60 << 20
        ),
        cost_estimate=pl.CostEstimate(
            flops=2 * rows * width * width, bytes_accessed=16 * rows * width, transcendentals=0
        ),
    )(x, blocks, stat, weight)


def backward_kernel(
    n, normed_ref, ghid_ref, head_ref, grad_ref, heads_ref,
    own, sib_out, sib_in, ring_out, ring_in, head_in, head_sum, head_all,
    ring_send, ring_recv, sib_send, sib_recv, head_sems,
):
    r = Ring(n)
    me, last = r.me, r.ring - 1
    enter(n, me)
    width = grad_ref.shape[1]
    cuts = pieces(grad_ref.shape[0])
    down = r.down()

    def product(owner, cols):
        return lax.dot_general(
            normed_ref[owner],
            ghid_ref[:, cols],
            (((0,), (0,)), ((), ())),
            preferred_element_type=jnp.float32,
        )

    def ring_copy(step, i):
        return remote(
            ring_out.at[step, cuts[i]], ring_in.at[step, cuts[i]],
            ring_send.at[step, i], ring_recv.at[step, i], down,
        )

    def sib_copy(step):
        return remote(
            sib_out.at[step], sib_in.at[step], sib_send.at[step], sib_recv.at[step], r.sibling
        )

    def terms(step):
        theirs = r.device(-r.step * (last - step), 1 - r.core)
        for j in range(0, width, TILE):
            cols = pl.ds(j, TILE)
            sib_out[step, :, cols] = product(theirs, cols).astype(jnp.bfloat16)
        sib_copy(step).start()
        mine = r.device(r.step * (last - step), r.core)
        for j in range(0, width, TILE):
            cols = pl.ds(j, TILE)
            own[:, cols] = product(mine, cols)
        sib_copy(step).wait_recv()

    terms(0)
    for i, cut in enumerate(cuts):
        ring_out[0, cut] = (own[cut] + sib_in[0, cut].astype(jnp.float32)).astype(jnp.bfloat16)
        ring_copy(0, i).start()
    spread(n, me, lambda peer: head_ref.at[peer], head_in, head_sems.at[0], head_sems.at[1])
    head_in[me] = head_ref[me]
    collect(n, head_in, head_sems.at[1])
    head_sum[...] = jnp.sum(head_in[...], 0)
    head_all[me] = head_sum[...]
    spread(n, me, lambda peer: head_sum, head_all, head_sems.at[2], head_sems.at[3])

    def hop(step, _):
        terms(step)
        for i, cut in enumerate(cuts):
            ring_copy(step - 1, i).wait_recv()
            ring_out[step, cut] = (
                own[cut]
                + sib_in[step, cut].astype(jnp.float32)
                + ring_in[step - 1, cut].astype(jnp.float32)
            ).astype(jnp.bfloat16)
            ring_copy(step, i).start()
        return 0

    lax.fori_loop(1, last, hop, 0)
    terms(last)
    for i, cut in enumerate(cuts):
        ring_copy(last - 1, i).wait_recv()
        grad_ref[cut] = (
            own[cut]
            + sib_in[last, cut].astype(jnp.float32)
            + ring_in[last - 1, cut].astype(jnp.float32)
        )
    collect(n, head_all, head_sems.at[3])
    heads_ref[...] = head_all[...]
    collect(n, head_in, head_sems.at[0])
    collect(n, head_all, head_sems.at[2])

    def drain(step, _):
        sib_copy(step).wait_send()

        @pl.when(step < last)
        def _():
            for i in range(len(cuts)):
                ring_copy(step, i).wait_send()

        return 0

    lax.fori_loop(0, r.ring, drain, 0)


def backward(n, normed, ghid, head):
    rows, width = ghid.shape
    shard = normed.shape[1] // n
    blocks = normed.reshape(rows, n, shard).transpose(1, 0, 2)
    count = len(pieces(shard))
    ring = n // 2
    vmem = pl.BlockSpec(memory_space=pltpu.VMEM)
    sems = pltpu.SemaphoreType.DMA
    return pl.pallas_call(
        functools.partial(backward_kernel, n),
        name="backward",
        out_shape=(
            jax.ShapeDtypeStruct((shard, width), jnp.float32),
            jax.ShapeDtypeStruct(head.shape, jnp.float32),
        ),
        in_specs=[vmem, vmem, vmem],
        out_specs=(vmem, vmem),
        scratch_shapes=[
            pltpu.VMEM((shard, width), jnp.float32),
            pltpu.VMEM((ring, shard, width), jnp.bfloat16),
            pltpu.VMEM((ring, shard, width), jnp.bfloat16),
            pltpu.VMEM((ring - 1, shard, width), jnp.bfloat16),
            pltpu.VMEM((ring - 1, shard, width), jnp.bfloat16),
            pltpu.VMEM(head.shape, jnp.float32),
            pltpu.VMEM(head.shape[1:], jnp.float32),
            pltpu.VMEM(head.shape, jnp.float32),
            sems((ring - 1, count)),
            sems((ring - 1, count)),
            sems((ring,)),
            sems((ring,)),
            sems((4,)),
        ],
        compiler_params=pltpu.CompilerParams(
            collective_id=1, has_side_effects=True, vmem_limit_bytes=60 << 20
        ),
        cost_estimate=pl.CostEstimate(
            flops=2 * rows * width * width, bytes_accessed=32 * rows * width, transcendentals=0
        ),
    )(blocks, ghid, head)


def advantages(reward, value_old, done):
    keep = 1.0 - done.astype(jnp.float32)
    deltas = reward + GAMMA * value_old[:, 1:] * keep - value_old[:, :-1]

    def walk(carry, inputs):
        dstep, kstep = inputs
        carry = dstep + GAMMA * LAMBDA_GAE * kstep * carry
        return (carry, carry)

    start = jnp.zeros((reward.shape[0],), jnp.float32)
    _, stacked = lax.scan(walk, start, (deltas.T, keep.T), reverse=True)
    gae = stacked.T
    return (gae.reshape(-1), (gae + value_old[:, :-1]).reshape(-1))


def split3(value):
    first = lax.reduce_precision(value, 8, 7)
    second = lax.reduce_precision(value - first, 8, 7)
    third = value - first - second
    return [part.astype(jnp.bfloat16) for part in (first, second, third)]


def local(
    obs_feat,
    reward,
    value_old,
    done,
    minibatch_perm,
    old_mean,
    noise,
    gain_in,
    out_weight,
    head_weight,
    log_std,
):
    gae, returns = advantages(reward, value_old, done)
    local_rows, width = obs_feat.shape
    devices = lax.axis_size("fsdp")
    total_rows = local_rows * devices
    xf = obs_feat.astype(jnp.float32)
    normed = (xf * lax.rsqrt(jnp.mean(xf * xf, -1, keepdims=True) + NORM_EPS) * gain_in).astype(
        jnp.bfloat16
    )
    lane = lax.broadcasted_iota(jnp.int32, (8, 128), 1)
    stat = jnp.where(lane == 0, jnp.sum(gae), jnp.where(lane == 1, jnp.sum(gae * gae), 0.0))
    hidden, sums = forward(devices, obs_feat, normed, stat, out_weight)

    per_peer = local_rows // devices
    send_slot = minibatch_perm // local_rows * per_peer + minibatch_perm % per_peer
    place = (jnp.arange(local_rows)[:, None] == send_slot[None, :]).astype(jnp.bfloat16)
    send_hidden = jnp.dot(place, hidden.astype(jnp.bfloat16), preferred_element_type=jnp.bfloat16)
    hidden_out = lax.all_to_all(send_hidden, "fsdp", split_axis=0, concat_axis=0, tiled=True)

    mean_adv = sums[0, 0] / total_rows
    var_adv = sums[0, 1] / total_rows - mean_adv * mean_adv
    adv_b = ((gae - mean_adv) * lax.rsqrt(var_adv + NORM_EPS)).astype(jnp.bfloat16)
    ret_b = returns.astype(jnp.bfloat16)
    scale = 1.0 / jnp.sqrt(jnp.float32(total_rows))
    rinv = lax.rsqrt(jnp.mean(hidden * hidden, -1, keepdims=True) + NORM_EPS)
    hnorm = hidden * rinv
    hnorm_b = hnorm.astype(jnp.bfloat16)
    heads = jnp.dot(hnorm_b, head_weight, preferred_element_type=jnp.float32)
    nact = log_std.shape[0]
    mean_act = heads[:, :nact]
    value = heads[:, nact]
    std_dev = jnp.exp(log_std)
    offset = old_mean.astype(jnp.float32) - mean_act
    sample = noise.astype(jnp.float32)
    logr = jnp.sum(-sample * offset / std_dev - offset * offset / (2.0 * std_dev * std_dev), -1)
    ratio = jnp.exp(logr)
    advant = adv_b.astype(jnp.float32)
    clipped = jnp.clip(ratio, 1.0 - CLIP_EPS, 1.0 + CLIP_EPS)
    active = ratio * advant <= clipped * advant
    gratio = jnp.where(active, -scale * advant, 0.0)
    glogr = gratio * ratio
    gmean = glogr[:, None] * (sample / std_dev + offset / (std_dev * std_dev))
    gvalue = scale * (value - ret_b.astype(jnp.float32))
    std_local = jnp.sum(
        glogr[:, None] * (sample * offset / std_dev + offset * offset / (std_dev * std_dev)), 0
    )
    ghead = jnp.concatenate([gmean, gvalue[:, None]], 1)
    parts = split3(ghead)
    head_local = sum(
        lax.dot_general(part, hnorm_b, (((0,), (0,)), ((), ())), preferred_element_type=jnp.float32)
        for part in parts
    )
    ghn = sum(
        lax.dot_general(part, head_weight, (((1,), (1,)), ((), ())), preferred_element_type=jnp.float32)
        for part in parts
    )
    ghid = rinv * (ghn - hnorm * jnp.mean(ghn * hnorm, -1, keepdims=True))
    ghid_b = ghid.astype(jnp.bfloat16)

    share = width // devices
    block = jnp.zeros((devices, 16, share), jnp.float32)
    block = block.at[:, : nact + 1].set(head_local.reshape(nact + 1, devices, share).swapaxes(0, 1))
    block = block.at[:, nact + 1, :nact].set(std_local)
    grad_weight, heads_all = backward(devices, normed, ghid_b, block)
    grad_head = heads_all[:, : nact + 1].swapaxes(0, 1).reshape(nact + 1, width).T
    grad_std = heads_all[0, nact + 1, :nact]
    return (hidden_out, grad_weight, grad_head, grad_std)


def solution(mesh):
    return jax.shard_map(
        local,
        mesh=mesh,
        in_specs=(
            P(("groups", "fsdp"), None),
            P(("groups", "fsdp"), None),
            P(("groups", "fsdp"), None),
            P(("groups", "fsdp"), None),
            P(("groups", "fsdp")),
            P(("groups", "fsdp"), None),
            P(("groups", "fsdp"), None),
            P(),
            P("fsdp", None),
            P(),
            P(),
        ),
        out_specs=(
            P(("groups", "fsdp"), None),
            P(("groups", "fsdp"), None),
            P("groups", None),
            P("groups"),
        ),
        check_vma=False,
    )
```

```python
import functools

import jax
import jax.numpy as jnp
from jax import lax
from jax.experimental import pallas as pl
from jax.experimental.pallas import tpu as pltpu
from jax.sharding import PartitionSpec as P

GAMMA = 0.99
LAMBDA_GAE = 0.95
CLIP_EPS = 0.2
NORM_EPS = 1e-05
MESH = pl.DeviceIdType.MESH
TILE = 512
STRIP = 128


def chip_at(pos, ring):
    half = ring // 2
    col = pos // half
    row = col * (ring - 1 - pos) + (1 - col) * pos
    return 2 * row + col


class Ring:
    def __init__(self, n):
        self.n = n
        self.me = lax.axis_index("fsdp")
        self.ring = n // 2
        self.core = lax.rem(self.me, 2)
        chip = self.me // 2
        col = lax.rem(chip, 2)
        row = chip // 2
        self.pos = col * (self.ring - 1 - row) + (1 - col) * row
        self.step = 1 - 2 * self.core
        self.sibling = self.me + self.step

    def device(self, ahead, core):
        pos = lax.rem(self.pos + ahead + self.ring, self.ring)
        return 2 * chip_at(pos, self.ring) + core

    def down(self):
        return self.device(self.step, self.core)


def enter(n, me):
    barrier = pltpu.get_barrier_semaphore()

    @pl.loop(1, n)
    def _(k):
        pl.semaphore_signal(
            barrier, inc=1, device_id={"fsdp": lax.rem(me + k, n)}, device_id_type=MESH
        )

    pl.semaphore_wait(barrier, n - 1)


def remote(src, dst, send, recv, device):
    return pltpu.make_async_remote_copy(
        src_ref=src,
        dst_ref=dst,
        send_sem=send,
        recv_sem=recv,
        device_id={"fsdp": device},
        device_id_type=MESH,
    )


def pieces(rows):
    count = 2 if rows % 32 == 0 else 1
    return [pl.ds(i * (rows // count), rows // count) for i in range(count)]


def spread(n, me, source_of, dst, send, recv):
    @pl.loop(1, n)
    def _(k):
        peer = lax.rem(me + k, n)
        remote(source_of(peer), dst.at[me], send, recv, peer).start()


def collect(n, slots, sem):
    part = slots.at[pl.ds(0, n - 1)]
    pltpu.make_async_copy(part, part, sem).wait()


def step_kernel(
    n, nact, per, burst, aligned,
    x_ref, lhs_ref, w_ref, gain_ref, gae_ref, ret_ref, slot_ref, mean_ref, noise_ref, head_ref, std_ref,
    out_ref, grad_ref, heads_ref,
    normed, held, hidden, hidden_b, hnorm_b, rinv, ghid, ghead, ghead3, ordered,
    stat, stats, own, sib_out, sib_in, ring_out, ring_in, head_out, head_in, head_sum, head_all,
    local_sem, gat_send, gat_recv, gsib_send, gsib_recv,
    ring_send, ring_recv, sib_send, sib_recv, small_sems,
):
    r = Ring(n)
    me, last = r.me, r.ring - 1
    rows, width = x_ref.shape
    shard = w_ref.shape[0]
    first = pltpu.make_async_copy(w_ref, held.at[me], local_sem.at[0])
    first.start()
    gae = gae_ref[...]
    lane = lax.broadcasted_iota(jnp.int32, stat.shape, 1)
    stat[...] = jnp.where(
        lane == 0,
        jnp.sum(gae, axis=1, keepdims=True),
        jnp.where(lane == 1, jnp.sum(gae * gae, axis=1, keepdims=True), 0.0),
    )
    enter(n, me)
    cuts = pieces(shard)
    down = r.down()

    def gather_copy(owner, step, i):
        part = held.at[owner, cuts[i]]
        return remote(part, part, gat_send.at[step, i], gat_recv.at[step, i], down)

    def gather_sib(owner, step, i):
        part = held.at[owner, cuts[i]]
        return remote(part, part, gsib_send.at[step, i], gsib_recv.at[step, i], r.sibling)

    def mine(step):
        return r.device(-r.step * step, r.core)

    def theirs(step):
        return r.device(r.step * step, 1 - r.core)

    def columns(owner):
        if not aligned:
            return lhs_ref[owner]
        return normed[:, pl.ds(pl.multiple_of(owner * shard, shard), shard)]

    def add(owner):
        left = columns(owner)
        for j in range(0, width, TILE):
            cols = pl.ds(j, TILE)
            hidden[:, cols] += jnp.dot(
                left, held[owner, :, cols], preferred_element_type=jnp.float32
            )

    first.wait()
    for i in range(len(cuts)):
        gather_copy(me, 1, i).start()
        gather_sib(me, 0, i).start()
    spread(n, me, lambda peer: stat, stats, small_sems.at[4], small_sems.at[5])
    stats[me] = stat[...]

    @pl.loop(0, rows // STRIP)
    def _(t):
        strip = pl.ds(pl.multiple_of(t * STRIP, STRIP), STRIP)
        xf = x_ref[strip].astype(jnp.float32)
        hidden[strip] = xf
        if aligned:
            scale = lax.rsqrt(jnp.mean(xf * xf, -1, keepdims=True) + NORM_EPS)
            normed[strip] = (xf * scale * gain_ref[...]).astype(jnp.bfloat16)

    def gather_hop(step, _):
        owner = mine(step)
        for i in range(len(cuts)):
            gather_copy(owner, step, i).wait_recv()

            @pl.when(step < last)
            def _():
                gather_copy(owner, step + 1, i).start()

            gather_sib(owner, step, i).start()
            if i == 0:
                add(mine(step - 1))
        for i in range(len(cuts)):
            gather_sib(theirs(step - 1), step - 1, i).wait_recv()
        add(theirs(step - 1))
        return 0

    lax.fori_loop(1, r.ring, gather_hop, 0)
    add(mine(last))
    for i in range(len(cuts)):
        gather_sib(theirs(last), last, i).wait_recv()
    add(theirs(last))

    @pl.loop(0, rows // STRIP)
    def _(t):
        strip = pl.ds(pl.multiple_of(t * STRIP, STRIP), STRIP)
        h = hidden[strip]
        hidden_b[strip] = h.astype(jnp.bfloat16)
        scale = lax.rsqrt(jnp.mean(h * h, -1, keepdims=True) + NORM_EPS)
        rinv[strip] = scale
        hnorm_b[strip] = (h * scale).astype(jnp.bfloat16)

    slots = n * per
    place = (
        lax.broadcasted_iota(jnp.int32, (slots, rows), 0)
        == jnp.broadcast_to(slot_ref[...], (slots, rows))
    ).astype(jnp.float32).astype(jnp.bfloat16)
    for j in range(0, width, TILE):
        cols = pl.ds(j, TILE)
        moved = jnp.dot(place, hidden_b[:, cols], preferred_element_type=jnp.float32)
        ordered[:, :, cols] = moved.reshape(n, per, TILE).astype(jnp.bfloat16)

    def row_copy(peer):
        return remote(ordered.at[peer], out_ref.at[me], small_sems.at[6], small_sems.at[7], peer)

    @pl.loop(1, burst)
    def _(k):
        row_copy(lax.rem(me + k, n)).start()

    def more_rows(step):
        for u in range(2):
            k = burst + 2 * step + u

            @pl.when(k < n)
            def _():
                row_copy(lax.rem(me + k, n)).start()

    kept = pltpu.make_async_copy(ordered.at[me], out_ref.at[me], local_sem.at[1])
    kept.start()

    collect(n, stats, small_sems.at[5])
    sums = jnp.sum(stats[...], 0)
    total_rows = rows * n
    mean_adv = sums[0:1, 0:1] / total_rows
    var_adv = sums[0:1, 1:2] / total_rows - mean_adv * mean_adv
    advant = ((gae - mean_adv) * lax.rsqrt(var_adv + NORM_EPS)).astype(jnp.bfloat16).astype(jnp.float32)
    returns = ret_ref[...].astype(jnp.bfloat16).astype(jnp.float32)
    scale = 1.0 / jnp.sqrt(jnp.full((1, 1), total_rows, jnp.float32))
    heads = lax.dot_general(
        head_ref[0:16], hnorm_b[...], (((1,), (1,)), ((), ())), preferred_element_type=jnp.float32
    )
    std_dev = jnp.exp(std_ref[...])
    offset = mean_ref[...].astype(jnp.float32) - heads[0:nact]
    sample = noise_ref[...].astype(jnp.float32)
    logr = jnp.sum(
        -sample * offset / std_dev - offset * offset / (2.0 * std_dev * std_dev), 0, keepdims=True
    )
    ratio = jnp.exp(logr)
    clipped = jnp.clip(ratio, 1.0 - CLIP_EPS, 1.0 + CLIP_EPS)
    gratio = jnp.where(ratio * advant <= clipped * advant, -scale * advant, 0.0)
    glogr = gratio * ratio
    ghead[...] = jnp.zeros_like(ghead)
    ghead[0:nact] = glogr * (sample / std_dev + offset / (std_dev * std_dev))
    ghead[nact : nact + 1] = scale * (heads[nact : nact + 1] - returns)
    std_local = jnp.sum(
        glogr * (sample * offset / std_dev + offset * offset / (std_dev * std_dev)), 1, keepdims=True
    )
    rest = ghead[...]
    for k in range(3):
        term = rest.astype(jnp.bfloat16)
        ghead3[16 * k : 16 * k + 16] = term
        rest = rest - term.astype(jnp.float32)

    @pl.loop(0, rows // STRIP)
    def _(t):
        strip = pl.ds(pl.multiple_of(t * STRIP, STRIP), STRIP)
        ghn = lax.dot_general(
            ghead3[:, strip], head_ref[...], (((0,), (0,)), ((), ())),
            preferred_element_type=jnp.float32,
        )
        hnorm = hidden[strip] * rinv[strip]
        inner = jnp.mean(ghn * hnorm, -1, keepdims=True)
        ghid[strip] = (rinv[strip] * (ghn - hnorm * inner)).astype(jnp.bfloat16)

    def product(owner, cols):
        return lax.dot_general(
            columns(owner), ghid[:, cols], (((0,), (0,)), ((), ())),
            preferred_element_type=jnp.float32,
        )

    def ring_copy(step, i):
        return remote(
            ring_out.at[step, cuts[i]], ring_in.at[step, cuts[i]],
            ring_send.at[step, i], ring_recv.at[step, i], down,
        )

    def sib_copy(step):
        return remote(
            sib_out.at[step], sib_in.at[step], sib_send.at[step], sib_recv.at[step], r.sibling
        )

    def terms(step):
        other = r.device(-r.step * (last - step), 1 - r.core)
        for j in range(0, width, TILE):
            cols = pl.ds(j, TILE)
            sib_out[step, :, cols] = product(other, cols).astype(jnp.bfloat16)
        sib_copy(step).start()
        target = r.device(r.step * (last - step), r.core)
        for j in range(0, width, TILE):
            cols = pl.ds(j, TILE)
            own[:, cols] = product(target, cols)
        sib_copy(step).wait_recv()

    terms(0)
    for i, cut in enumerate(cuts):
        ring_out[0, cut] = (own[cut] + sib_in[0, cut].astype(jnp.float32)).astype(jnp.bfloat16)
        ring_copy(0, i).start()
    more_rows(0)

    head_local = jnp.dot(ghead3[...], hnorm_b[...], preferred_element_type=jnp.float32)
    head_local = head_local[0:16] + head_local[16:32] + head_local[32:48]
    share = width // n
    diagonal = lax.broadcasted_iota(jnp.int32, (nact, share), 0) == lax.broadcasted_iota(
        jnp.int32, (nact, share), 1
    )
    std_row = jnp.sum(jnp.where(diagonal, std_local, 0.0), 0, keepdims=True)
    line = lax.broadcasted_iota(jnp.int32, (16, share), 0)
    for j in range(n):
        head_out[j] = jnp.where(
            line == nact + 1, std_row, head_local[:, j * share : (j + 1) * share]
        )
    spread(n, me, lambda peer: head_out.at[peer], head_in, small_sems.at[0], small_sems.at[1])
    head_in[me] = head_out[me]

    def hop(step, _):
        terms(step)
        for i, cut in enumerate(cuts):
            ring_copy(step - 1, i).wait_recv()
            ring_out[step, cut] = (
                own[cut]
                + sib_in[step, cut].astype(jnp.float32)
                + ring_in[step - 1, cut].astype(jnp.float32)
            ).astype(jnp.bfloat16)
            ring_copy(step, i).start()
        more_rows(step)
        return 0

    lax.fori_loop(1, r.ring // 2, hop, 0)
    collect(n, head_in, small_sems.at[1])
    head_sum[...] = jnp.sum(head_in[...], 0)
    head_all[me] = head_sum[...]
    spread(n, me, lambda peer: head_sum, head_all, small_sems.at[2], small_sems.at[3])
    lax.fori_loop(r.ring // 2, last, hop, 0)
    terms(last)
    more_rows(last)
    for i, cut in enumerate(cuts):
        ring_copy(last - 1, i).wait_recv()
        grad_ref[cut] = (
            own[cut]
            + sib_in[last, cut].astype(jnp.float32)
            + ring_in[last - 1, cut].astype(jnp.float32)
        )
    collect(n, head_all, small_sems.at[3])
    heads_ref[...] = head_all[...]
    kept.wait()
    collect(n, out_ref, small_sems.at[7])
    collect(n, ordered, small_sems.at[6])
    collect(n, stats, small_sems.at[4])
    collect(n, head_in, small_sems.at[0])
    collect(n, head_all, small_sems.at[2])

    def drain(step, _):
        owner = mine(step)
        for i in range(len(cuts)):
            @pl.when(step < last)
            def _():
                gather_copy(owner, step + 1, i).wait_send()
                ring_copy(step, i).wait_send()

            gather_sib(owner, step, i).wait_send()
        sib_copy(step).wait_send()
        return 0

    lax.fori_loop(0, r.ring, drain, 0)


def step_call(n, x, weight, gain, gae, ret, slot, old_mean, noise, head, log_std):
    rows, width = x.shape
    shard = weight.shape[0]
    nact = log_std.shape[0]
    per = -(-(rows // n) // 8) * 8
    aligned = shard % 128 == 0
    blocks = jnp.zeros((8, 128), jnp.bfloat16)
    if not aligned:
        xf = x.astype(jnp.float32)
        normed = xf * lax.rsqrt(jnp.mean(xf * xf, -1, keepdims=True) + NORM_EPS) * gain
        blocks = normed.astype(jnp.bfloat16).reshape(rows, n, shard).transpose(1, 0, 2)
    count = len(pieces(shard))
    ring = n // 2
    share = width // n
    vmem = pl.BlockSpec(memory_space=pltpu.VMEM)
    anywhere = pl.BlockSpec(memory_space=pl.ANY)
    sems = pltpu.SemaphoreType.DMA
    bf16, f32 = jnp.bfloat16, jnp.float32
    return pl.pallas_call(
        functools.partial(step_kernel, n, nact, per, max(n // 4, 1), aligned),
        name="step",
        out_shape=(
            jax.ShapeDtypeStruct((n, per, width), bf16),
            jax.ShapeDtypeStruct((shard, width), f32),
            jax.ShapeDtypeStruct((n, 16, share), f32),
        ),
        in_specs=[vmem, vmem, anywhere] + [vmem] * 8,
        out_specs=(anywhere, vmem, vmem),
        scratch_shapes=[
            pltpu.VMEM((rows, width) if aligned else (16, 128), bf16),
            pltpu.VMEM((n, shard, width), bf16),
            pltpu.VMEM((rows, width), f32),
            pltpu.VMEM((rows, width), bf16),
            pltpu.VMEM((rows, width), bf16),
            pltpu.VMEM((rows, 1), f32),
            pltpu.VMEM((rows, width), bf16),
            pltpu.VMEM((16, rows), f32),
            pltpu.VMEM((48, rows), bf16),
            pltpu.VMEM((n, per, width), bf16),
            pltpu.VMEM((8, 128), f32),
            pltpu.VMEM((n, 8, 128), f32),
            pltpu.VMEM((shard, width), f32),
            pltpu.VMEM((ring, shard, width), bf16),
            pltpu.VMEM((ring, shard, width), bf16),
            pltpu.VMEM((ring - 1, shard, width), bf16),
            pltpu.VMEM((ring - 1, shard, width), bf16),
            pltpu.VMEM((n, 16, share), f32),
            pltpu.VMEM((n, 16, share), f32),
            pltpu.VMEM((16, share), f32),
            pltpu.VMEM((n, 16, share), f32),
            sems((2,)),
            sems((ring, count)),
            sems((ring, count)),
            sems((ring, count)),
            sems((ring, count)),
            sems((ring - 1, count)),
            sems((ring - 1, count)),
            sems((ring,)),
            sems((ring,)),
            sems((8,)),
        ],
        compiler_params=pltpu.CompilerParams(
            collective_id=0, has_side_effects=True, vmem_limit_bytes=66_000_000
        ),
        cost_estimate=pl.CostEstimate(
            flops=4 * rows * width * width, bytes_accessed=32 * rows * width, transcendentals=0
        ),
    )(x, blocks, weight, gain[None], gae, ret, slot, old_mean, noise, head, log_std[:, None])


def advantages(reward, value_old, done):
    keep = 1.0 - done.astype(jnp.float32)
    deltas = reward + GAMMA * value_old[:, 1:] * keep - value_old[:, :-1]

    carry = jnp.zeros((reward.shape[0],), jnp.float32)
    column = []
    for t in reversed(range(reward.shape[1])):
        carry = deltas[:, t] + GAMMA * LAMBDA_GAE * keep[:, t] * carry
        column.append(carry)
    gae = jnp.stack(column[::-1], 1)
    return (gae.reshape(-1), (gae + value_old[:, :-1]).reshape(-1))


def local(
    obs_feat,
    reward,
    value_old,
    done,
    minibatch_perm,
    old_mean,
    noise,
    gain_in,
    out_weight,
    head_weight,
    log_std,
):
    gae, returns = advantages(reward, value_old, done)
    local_rows, width = obs_feat.shape
    devices = lax.axis_size("fsdp")
    nact = log_std.shape[0]
    per_peer = local_rows // devices
    padded = -(-per_peer // 8) * 8
    slot = minibatch_perm // local_rows * padded + minibatch_perm % per_peer
    head = jnp.pad(head_weight.T, ((0, 16 - head_weight.shape[1]), (0, 0)))
    moved, grad_weight, heads_all = step_call(
        devices, obs_feat, out_weight, gain_in, gae[None], returns[None], slot[None],
        old_mean.T, noise.T, jnp.tile(head, (3, 1)), log_std,
    )
    hidden_out = moved[:, :per_peer].reshape(local_rows, width)
    grad_head = heads_all[:, : nact + 1].swapaxes(0, 1).reshape(nact + 1, width).T
    grad_std = heads_all[0, nact + 1, :nact]
    return (hidden_out, grad_weight, grad_head, grad_std)


def solution(mesh):
    return jax.shard_map(
        local,
        mesh=mesh,
        in_specs=(
            P(("groups", "fsdp"), None),
            P(("groups", "fsdp"), None),
            P(("groups", "fsdp"), None),
            P(("groups", "fsdp"), None),
            P(("groups", "fsdp")),
            P(("groups", "fsdp"), None),
            P(("groups", "fsdp"), None),
            P(),
            P("fsdp", None),
            P(),
            P(),
        ),
        out_specs=(
            P(("groups", "fsdp"), None),
            P(("groups", "fsdp"), None),
            P("groups", None),
            P("groups"),
        ),
        check_vma=False,
    )
```

```python
import functools

import jax
import jax.numpy as jnp
from jax import lax
from jax.experimental import pallas as pl
from jax.experimental.pallas import tpu as pltpu
from jax.sharding import PartitionSpec as P

GAMMA = 0.99
LAMBDA_GAE = 0.95
CLIP_EPS = 0.2
NORM_EPS = 1e-05
MESH = pl.DeviceIdType.MESH
TILE = 512
STRIP = 128


def chip_at(pos, ring):
    half = ring // 2
    col = pos // half
    row = col * (ring - 1 - pos) + (1 - col) * pos
    return 2 * row + col


class Ring:
    def __init__(self, n):
        self.n = n
        self.me = lax.axis_index("fsdp")
        self.ring = n // 2
        self.core = lax.rem(self.me, 2)
        chip = self.me // 2
        col = lax.rem(chip, 2)
        row = chip // 2
        self.pos = col * (self.ring - 1 - row) + (1 - col) * row
        self.step = 1 - 2 * self.core
        self.sibling = self.me + self.step

    def device(self, ahead, core):
        pos = lax.rem(self.pos + ahead + self.ring, self.ring)
        return 2 * chip_at(pos, self.ring) + core

    def down(self):
        return self.device(self.step, self.core)


def enter(n, me, twin):
    barrier = pltpu.get_barrier_semaphore()
    if twin is not None:
        pl.semaphore_signal(barrier, inc=1, device_id=twin, device_id_type=MESH)

    @pl.loop(1, n)
    def _(k):
        pl.semaphore_signal(
            barrier, inc=1, device_id={"fsdp": lax.rem(me + k, n)}, device_id_type=MESH
        )

    pl.semaphore_wait(barrier, n - 1 + (twin is not None))


def remote(src, dst, send, recv, device):
    return pltpu.make_async_remote_copy(
        src_ref=src,
        dst_ref=dst,
        send_sem=send,
        recv_sem=recv,
        device_id=device if isinstance(device, dict) else {"fsdp": device},
        device_id_type=MESH,
    )


def pieces(rows):
    count = 2 if rows % 32 == 0 else 1
    return [pl.ds(i * (rows // count), rows // count) for i in range(count)]


def spread(n, me, source_of, dst, send, recv):
    @pl.loop(1, n)
    def _(k):
        peer = lax.rem(me + k, n)
        remote(source_of(peer), dst.at[me], send, recv, peer).start()


def collect(n, slots, sem):
    part = slots.at[pl.ds(0, n - 1)]
    pltpu.make_async_copy(part, part, sem).wait()


def step_kernel(
    n, nact, per, burst, aligned, twinned,
    x_ref, w_ref, gain_ref, adv_ref, slot_ref, mean_ref, noise_ref, weight_ref, std_ref, lhs_ref,
    out_ref, grad_ref, heads_ref,
    normed, held, hidden, hidden_b, hnorm_b, rinv, ghid, ghead, ghead3, ordered,
    stat, stats, own, sib_out, sib_in, ring_out, ring_in, head_out, head_in, head_sum, head_all,
    local_sem, gat_send, gat_recv, gsib_send, gsib_recv, twin_send, twin_recv, head_ref,
    ring_send, ring_recv, sib_send, sib_recv, small_sems,
):
    r = Ring(n)
    me, last = r.me, r.ring - 1
    rows, width = x_ref.shape
    shard = w_ref.shape[0]
    first = pltpu.make_async_copy(w_ref, held.at[0, pl.ds(0, shard)], local_sem.at[0])
    first.start()
    gae = adv_ref[0:1]
    lane = lax.broadcasted_iota(jnp.int32, stat.shape, 1)
    stat[...] = jnp.where(
        lane == 0,
        jnp.sum(gae, axis=1, keepdims=True),
        jnp.where(lane == 1, jnp.sum(gae * gae, axis=1, keepdims=True), 0.0),
    )
    twin = None
    group = lax.axis_index("groups")
    if twinned:
        twin = {"groups": 1 - group, "fsdp": me}
    enter(n, me, twin)
    cuts = pieces(shard)
    down = r.down()

    if twinned:
        half, quarter = shard // 2, shard // 4
        mid = pl.multiple_of(half + quarter * group, quarter)
        far = pl.multiple_of(half + quarter * (1 - group), quarter)
        spans = [(0, half), (mid, quarter), (far, quarter)]
    else:
        spans = [(0, shard)]
    rung = spans[:2]

    def gather_copy(step, i):
        start, size = spans[i]
        return remote(
            held.at[step - 1, pl.ds(start, size)], held.at[step, pl.ds(start, size)],
            gat_send.at[step, i], gat_recv.at[step, i], down,
        )

    def gather_sib(step, i):
        start, size = spans[i]
        return remote(
            held.at[step, pl.ds(start, size)], held.at[step, pl.ds(shard + start, size)],
            gsib_send.at[step, i], gsib_recv.at[step, i], r.sibling,
        )

    def gather_twin(step):
        part = held.at[step, pl.ds(*spans[1])]
        return remote(part, part, twin_send.at[step], twin_recv.at[step], twin)

    def from_twin(step):
        start, size = spans[2]
        part = held.at[step, pl.ds(start, size)]
        remote(part, part, twin_send.at[step], twin_recv.at[step], twin).wait_recv()
        gather_sib(step, 2).start()

    def mine(step):
        return r.device(-r.step * step, r.core)

    def theirs(step):
        return r.device(r.step * step, 1 - r.core)

    def columns(owner):
        if not aligned:
            return lhs_ref[owner]
        return normed[:, pl.ds(pl.multiple_of(owner * shard, shard), shard)]

    def add(step):
        for i in range(len(spans)):
            gather_sib(step, i).wait_recv()
        left = [columns(mine(step)), columns(theirs(step))]
        if aligned:
            left = [jnp.concatenate(left, 1)]
        deep = 2 * shard // len(left)
        for j in range(0, width, TILE):
            cols = pl.ds(j, TILE)
            hidden[:, cols] += sum(
                jnp.dot(
                    left[k], held[step, k * deep : (k + 1) * deep, cols],
                    preferred_element_type=jnp.float32,
                )
                for k in range(len(left))
            )

    first.wait()
    for i in range(len(spans)):
        if i < len(rung):
            gather_copy(1, i).start()
        gather_sib(0, i).start()
    head_ref[...] = jnp.zeros_like(head_ref)
    for k in range(3):
        head_ref[16 * k : 16 * k + nact + 1] = weight_ref[...]
    spread(n, me, lambda peer: stat, stats, small_sems.at[4], small_sems.at[5])
    stats[me] = stat[...]

    @pl.loop(0, rows // STRIP)
    def _(t):
        strip = pl.ds(pl.multiple_of(t * STRIP, STRIP), STRIP)
        xf = x_ref[strip].astype(jnp.float32)
        hidden[strip] = xf
        if aligned:
            scale = lax.rsqrt(jnp.mean(xf * xf, -1, keepdims=True) + NORM_EPS)
            normed[strip] = (xf * scale * gain_ref[...]).astype(jnp.bfloat16)

    def gather_hop(step, _):
        for i in range(len(rung)):
            gather_copy(step, i).wait_recv()

            @pl.when(step < last)
            def _():
                gather_copy(step + 1, i).start()

            gather_sib(step, i).start()
            if i == 1:
                gather_twin(step).start()
            elif twinned:
                @pl.when(step > 1)
                def _():
                    from_twin(step - 1)
        add(step - 1)
        return 0

    lax.fori_loop(1, r.ring, gather_hop, 0)
    if twinned:
        from_twin(last)
    add(last)

    @pl.loop(0, rows // STRIP)
    def _(t):
        strip = pl.ds(pl.multiple_of(t * STRIP, STRIP), STRIP)
        h = hidden[strip]
        hidden_b[strip] = h.astype(jnp.bfloat16)
        scale = lax.rsqrt(jnp.mean(h * h, -1, keepdims=True) + NORM_EPS)
        rinv[strip] = scale
        hnorm_b[strip] = (h * scale).astype(jnp.bfloat16)

    slots = n * per
    place = (
        lax.broadcasted_iota(jnp.int32, (slots, rows), 0)
        == jnp.broadcast_to(slot_ref[...], (slots, rows))
    ).astype(jnp.float32).astype(jnp.bfloat16)
    for j in range(0, width, TILE):
        cols = pl.ds(j, TILE)
        moved = jnp.dot(place, hidden_b[:, cols], preferred_element_type=jnp.float32)
        ordered[:, :, cols] = moved.reshape(n, per, TILE).astype(jnp.bfloat16)

    def row_copy(peer):
        return remote(ordered.at[peer], out_ref.at[me], small_sems.at[6], small_sems.at[7], peer)

    @pl.loop(1, burst)
    def _(k):
        row_copy(lax.rem(me + k, n)).start()

    def more_rows(step):
        for u in range(2):
            k = burst + 2 * step + u

            @pl.when(k < n)
            def _():
                row_copy(lax.rem(me + k, n)).start()

    kept = pltpu.make_async_copy(ordered.at[me], out_ref.at[me], local_sem.at[1])
    kept.start()

    collect(n, stats, small_sems.at[5])
    sums = jnp.sum(stats[...], 0)
    total_rows = rows * n
    mean_adv = sums[0:1, 0:1] / total_rows
    var_adv = sums[0:1, 1:2] / total_rows - mean_adv * mean_adv
    advant = ((gae - mean_adv) * lax.rsqrt(var_adv + NORM_EPS)).astype(jnp.bfloat16).astype(jnp.float32)
    returns = adv_ref[1:2].astype(jnp.bfloat16).astype(jnp.float32)
    scale = 1.0 / jnp.sqrt(jnp.full((1, 1), total_rows, jnp.float32))
    heads = lax.dot_general(
        head_ref[0:16], hnorm_b[...], (((1,), (1,)), ((), ())), preferred_element_type=jnp.float32
    )
    square = (nact, nact)
    diagonal = lax.broadcasted_iota(jnp.int32, square, 0) == lax.broadcasted_iota(jnp.int32, square, 1)
    std_dev = jnp.exp(
        jnp.sum(jnp.where(diagonal, jnp.broadcast_to(std_ref[...], square), 0.0), 1, keepdims=True)
    )
    offset = mean_ref[...].astype(jnp.float32) - heads[0:nact]
    sample = noise_ref[...].astype(jnp.float32)
    logr = jnp.sum(
        -sample * offset / std_dev - offset * offset / (2.0 * std_dev * std_dev), 0, keepdims=True
    )
    ratio = jnp.exp(logr)
    clipped = jnp.clip(ratio, 1.0 - CLIP_EPS, 1.0 + CLIP_EPS)
    gratio = jnp.where(ratio * advant <= clipped * advant, -scale * advant, 0.0)
    glogr = gratio * ratio
    ghead[...] = jnp.zeros_like(ghead)
    ghead[0:nact] = glogr * (sample / std_dev + offset / (std_dev * std_dev))
    ghead[nact : nact + 1] = scale * (heads[nact : nact + 1] - returns)
    std_local = jnp.sum(
        glogr * (sample * offset / std_dev + offset * offset / (std_dev * std_dev)), 1, keepdims=True
    )
    rest = ghead[...]
    for k in range(3):
        term = rest.astype(jnp.bfloat16)
        ghead3[16 * k : 16 * k + 16] = term
        rest = rest - term.astype(jnp.float32)

    @pl.loop(0, rows // STRIP)
    def _(t):
        strip = pl.ds(pl.multiple_of(t * STRIP, STRIP), STRIP)
        ghn = lax.dot_general(
            ghead3[:, strip], head_ref[...], (((0,), (0,)), ((), ())),
            preferred_element_type=jnp.float32,
        )
        hnorm = hidden[strip] * rinv[strip]
        inner = jnp.mean(ghn * hnorm, -1, keepdims=True)
        ghid[strip] = (rinv[strip] * (ghn - hnorm * inner)).astype(jnp.bfloat16)

    def product(owner, cols):
        return lax.dot_general(
            columns(owner), ghid[:, cols], (((0,), (0,)), ((), ())),
            preferred_element_type=jnp.float32,
        )

    def ring_copy(step, i):
        return remote(
            ring_out.at[step, cuts[i]], ring_in.at[step, cuts[i]],
            ring_send.at[step, i], ring_recv.at[step, i], down,
        )

    def sib_copy(step):
        return remote(
            sib_out.at[step], sib_in.at[step], sib_send.at[step], sib_recv.at[step], r.sibling
        )

    def terms(step):
        other = r.device(-r.step * (last - step), 1 - r.core)
        for j in range(0, width, TILE):
            cols = pl.ds(j, TILE)
            sib_out[step, :, cols] = product(other, cols).astype(jnp.bfloat16)
        sib_copy(step).start()
        target = r.device(r.step * (last - step), r.core)
        for j in range(0, width, TILE):
            cols = pl.ds(j, TILE)
            own[:, cols] = product(target, cols)
        sib_copy(step).wait_recv()

    terms(0)
    for i, cut in enumerate(cuts):
        ring_out[0, cut] = (own[cut] + sib_in[0, cut].astype(jnp.float32)).astype(jnp.bfloat16)
        ring_copy(0, i).start()
    more_rows(0)

    head_local = jnp.dot(ghead3[...], hnorm_b[...], preferred_element_type=jnp.float32)
    head_local = head_local[0:16] + head_local[16:32] + head_local[32:48]
    share = width // n
    diagonal = lax.broadcasted_iota(jnp.int32, (nact, share), 0) == lax.broadcasted_iota(
        jnp.int32, (nact, share), 1
    )
    std_row = jnp.sum(jnp.where(diagonal, std_local, 0.0), 0, keepdims=True)
    line = lax.broadcasted_iota(jnp.int32, (16, share), 0)
    for j in range(n):
        head_out[j] = jnp.where(
            line == nact + 1, std_row, head_local[:, j * share : (j + 1) * share]
        )
    spread(n, me, lambda peer: head_out.at[peer], head_in, small_sems.at[0], small_sems.at[1])
    head_in[me] = head_out[me]

    def hop(step, _):
        terms(step)
        for i, cut in enumerate(cuts):
            ring_copy(step - 1, i).wait_recv()
            ring_out[step, cut] = (
                own[cut]
                + sib_in[step, cut].astype(jnp.float32)
                + ring_in[step - 1, cut].astype(jnp.float32)
            ).astype(jnp.bfloat16)
            ring_copy(step, i).start()
        more_rows(step)
        return 0

    lax.fori_loop(1, r.ring // 2, hop, 0)
    collect(n, head_in, small_sems.at[1])
    head_sum[...] = jnp.sum(head_in[...], 0)
    head_all[me] = head_sum[...]
    spread(n, me, lambda peer: head_sum, head_all, small_sems.at[2], small_sems.at[3])
    lax.fori_loop(r.ring // 2, last, hop, 0)
    terms(last)
    more_rows(last)
    for i, cut in enumerate(cuts):
        ring_copy(last - 1, i).wait_recv()
        grad_ref[cut] = (
            own[cut]
            + sib_in[last, cut].astype(jnp.float32)
            + ring_in[last - 1, cut].astype(jnp.float32)
        )
    collect(n, head_all, small_sems.at[3])
    for j in range(n):
        heads_ref[:, j * share : (j + 1) * share] = head_all[j]
    kept.wait()
    collect(n, out_ref, small_sems.at[7])
    collect(n, ordered, small_sems.at[6])
    collect(n, stats, small_sems.at[4])
    collect(n, head_in, small_sems.at[0])
    collect(n, head_all, small_sems.at[2])

    def drain(step, _):
        for i in range(len(spans)):
            gather_sib(step, i).wait_send()
        for i in range(len(rung)):
            @pl.when(step < last)
            def _():
                gather_copy(step + 1, i).wait_send()

        for i in range(len(cuts)):
            @pl.when(step < last)
            def _():
                ring_copy(step, i).wait_send()

        if twinned:
            @pl.when(step > 0)
            def _():
                gather_twin(step).wait_send()

        sib_copy(step).wait_send()
        return 0

    lax.fori_loop(0, r.ring, drain, 0)


def step_call(n, groups, x, weight, gain, adv, slot, old_mean, noise, head, log_std):
    rows, width = x.shape
    shard = weight.shape[0]
    nact = log_std.shape[0]
    per = -(-(rows // n) // 8) * 8
    aligned = shard % 128 == 0
    twinned = groups == 2 and shard % 64 == 0
    blocks = []
    if not aligned:
        xf = x.astype(jnp.float32)
        normed = xf * lax.rsqrt(jnp.mean(xf * xf, -1, keepdims=True) + NORM_EPS) * gain
        blocks = [normed.astype(jnp.bfloat16).reshape(rows, n, shard).transpose(1, 0, 2)]
    count = len(pieces(shard))
    ring = n // 2
    share = width // n
    vmem = pl.BlockSpec(memory_space=pltpu.VMEM)
    anywhere = pl.BlockSpec(memory_space=pl.ANY)
    sems = pltpu.SemaphoreType.DMA
    bf16, f32 = jnp.bfloat16, jnp.float32
    fixed = functools.partial(step_kernel, n, nact, per, max(n // 4, 1), aligned, twinned)

    def body(*refs):
        given = 9
        lhs = refs[given] if blocks else None
        fixed(*refs[:given], lhs, *refs[given + len(blocks) :])

    return pl.pallas_call(
        body,
        name="step",
        out_shape=(
            jax.ShapeDtypeStruct((n, per, width), bf16),
            jax.ShapeDtypeStruct((shard, width), f32),
            jax.ShapeDtypeStruct((16, width), f32),
        ),
        in_specs=[vmem, anywhere] + [vmem] * (7 + len(blocks)),
        out_specs=(anywhere, vmem, vmem),
        scratch_shapes=[
            pltpu.VMEM((rows, width) if aligned else (16, 128), bf16),
            pltpu.VMEM((ring, 2 * shard, width), bf16),
            pltpu.VMEM((rows, width), f32),
            pltpu.VMEM((rows, width), bf16),
            pltpu.VMEM((rows, width), bf16),
            pltpu.VMEM((rows, 1), f32),
            pltpu.VMEM((rows, width), bf16),
            pltpu.VMEM((16, rows), f32),
            pltpu.VMEM((48, rows), bf16),
            pltpu.VMEM((n, per, width), bf16),
            pltpu.VMEM((8, 128), f32),
            pltpu.VMEM((n, 8, 128), f32),
            pltpu.VMEM((shard, width), f32),
            pltpu.VMEM((ring, shard, width), bf16),
            pltpu.VMEM((ring, shard, width), bf16),
            pltpu.VMEM((ring - 1, shard, width), bf16),
            pltpu.VMEM((ring - 1, shard, width), bf16),
            pltpu.VMEM((n, 16, share), f32),
            pltpu.VMEM((n, 16, share), f32),
            pltpu.VMEM((16, share), f32),
            pltpu.VMEM((n, 16, share), f32),
            sems((2,)),
            sems((ring, 2 if twinned else 1)),
            sems((ring, 2 if twinned else 1)),
            sems((ring, 3 if twinned else 1)),
            sems((ring, 3 if twinned else 1)),
            sems((ring if twinned else 1,)),
            sems((ring if twinned else 1,)),
            pltpu.VMEM((48, width), bf16),
            sems((ring - 1, count)),
            sems((ring - 1, count)),
            sems((ring,)),
            sems((ring,)),
            sems((8,)),
        ],
        compiler_params=pltpu.CompilerParams(
            collective_id=0, has_side_effects=True, vmem_limit_bytes=66_000_000
        ),
        cost_estimate=pl.CostEstimate(
            flops=4 * rows * width * width, bytes_accessed=32 * rows * width, transcendentals=0
        ),
    )(x, weight, gain[None], adv, slot, old_mean, noise, head, log_std[None], *blocks)


def advantages(reward, value_old, done):
    keep = 1.0 - done.astype(jnp.float32)
    deltas = reward + GAMMA * value_old[:, 1:] * keep - value_old[:, :-1]

    carry = jnp.zeros((reward.shape[0],), jnp.float32)
    column = []
    for t in reversed(range(reward.shape[1])):
        carry = deltas[:, t] + GAMMA * LAMBDA_GAE * keep[:, t] * carry
        column.append(carry)
    gae = jnp.stack(column[::-1], 1)
    return (gae.reshape(-1), (gae + value_old[:, :-1]).reshape(-1))


def local(
    obs_feat,
    reward,
    value_old,
    done,
    minibatch_perm,
    old_mean,
    noise,
    gain_in,
    out_weight,
    head_weight,
    log_std,
):
    gae, returns = advantages(reward, value_old, done)
    local_rows, width = obs_feat.shape
    devices = lax.axis_size("fsdp")
    nact = log_std.shape[0]
    per_peer = local_rows // devices
    padded = -(-per_peer // 8) * 8
    slot = minibatch_perm // local_rows * padded + minibatch_perm % per_peer
    moved, grad_weight, heads_all = step_call(
        devices, lax.axis_size("groups"), obs_feat, out_weight, gain_in, jnp.stack([gae, returns]),
        slot[None], old_mean.T, noise.T, head_weight.T, log_std,
    )
    hidden_out = moved[:, :per_peer].reshape(local_rows, width)
    grad_head = heads_all[: nact + 1].T
    grad_std = heads_all[nact + 1, :nact]
    return (hidden_out, grad_weight, grad_head, grad_std)


def solution(mesh):
    return jax.shard_map(
        local,
        mesh=mesh,
        in_specs=(
            P(("groups", "fsdp"), None),
            P(("groups", "fsdp"), None),
            P(("groups", "fsdp"), None),
            P(("groups", "fsdp"), None),
            P(("groups", "fsdp")),
            P(("groups", "fsdp"), None),
            P(("groups", "fsdp"), None),
            P(),
            P("fsdp", None),
            P(),
            P(),
        ),
        out_specs=(
            P(("groups", "fsdp"), None),
            P(("groups", "fsdp"), None),
            P("groups", None),
            P("groups"),
        ),
        check_vma=False,
    )
```

```python
import functools

import jax
import jax.numpy as jnp
from jax import lax
from jax.experimental import pallas as pl
from jax.experimental.pallas import tpu as pltpu
from jax.sharding import PartitionSpec as P

GAMMA = 0.99
LAMBDA_GAE = 0.95
CLIP_EPS = 0.2
NORM_EPS = 1e-05
MESH = pl.DeviceIdType.MESH
TILE = 512
STRIP = 128


def chip_at(pos, ring):
    half = ring // 2
    col = pos // half
    row = col * (ring - 1 - pos) + (1 - col) * pos
    return 2 * row + col


class Ring:
    def __init__(self, n):
        self.n = n
        self.me = lax.axis_index("fsdp")
        self.ring = n // 2
        self.core = lax.rem(self.me, 2)
        chip = self.me // 2
        col = lax.rem(chip, 2)
        row = chip // 2
        self.pos = col * (self.ring - 1 - row) + (1 - col) * row
        self.step = 1 - 2 * self.core
        self.sibling = self.me + self.step

    def device(self, ahead, core):
        pos = lax.rem(self.pos + ahead + self.ring, self.ring)
        return 2 * chip_at(pos, self.ring) + core

    def down(self):
        return self.device(self.step, self.core)


def enter(n, me, twin):
    barrier = pltpu.get_barrier_semaphore()
    if twin is not None:
        pl.semaphore_signal(barrier, inc=1, device_id=twin, device_id_type=MESH)

    @pl.loop(1, n)
    def _(k):
        pl.semaphore_signal(
            barrier, inc=1, device_id={"fsdp": lax.rem(me + k, n)}, device_id_type=MESH
        )

    pl.semaphore_wait(barrier, n - 1 + (twin is not None))


def remote(src, dst, send, recv, device):
    return pltpu.make_async_remote_copy(
        src_ref=src,
        dst_ref=dst,
        send_sem=send,
        recv_sem=recv,
        device_id=device if isinstance(device, dict) else {"fsdp": device},
        device_id_type=MESH,
    )


def pieces(rows):
    count = 2 if rows % 32 == 0 else 1
    return [pl.ds(i * (rows // count), rows // count) for i in range(count)]


def spread(n, me, source_of, dst, send, recv):
    @pl.loop(1, n)
    def _(k):
        peer = lax.rem(me + k, n)
        remote(source_of(peer), dst.at[me], send, recv, peer).start()


def collect(n, slots, sem):
    part = slots.at[pl.ds(0, n - 1)]
    pltpu.make_async_copy(part, part, sem).wait()


def step_kernel(
    n, nact, per, burst, aligned, twinned,
    x_ref, w_ref, gain_ref, adv_ref, slot_ref, mean_ref, noise_ref, weight_ref, std_ref, lhs_ref,
    out_ref, grad_ref, heads_ref,
    normed, held, hidden, hidden_b, hnorm_b, rinv, ghid, ghead, ghead3, ordered,
    stat, stats, own, sib_out, sib_in, ring_out, ring_in, head_out, head_in, head_sum, head_all,
    local_sem, gat_send, gat_recv, gsib_send, gsib_recv, twin_send, twin_recv, head_ref,
    ring_send, ring_recv, sib_send, sib_recv, small_sems,
):
    r = Ring(n)
    me, last = r.me, r.ring - 1
    rows, width = x_ref.shape
    shard = w_ref.shape[0]
    first = pltpu.make_async_copy(w_ref, held.at[0, pl.ds(0, shard)], local_sem.at[0])
    first.start()
    gae = adv_ref[0:1]
    lane = lax.broadcasted_iota(jnp.int32, stat.shape, 1)
    stat[...] = jnp.where(
        lane == 0,
        jnp.sum(gae, axis=1, keepdims=True),
        jnp.where(lane == 1, jnp.sum(gae * gae, axis=1, keepdims=True), 0.0),
    )
    twin = None
    group = lax.axis_index("groups")
    if twinned:
        twin = {"groups": 1 - group, "fsdp": me}
    enter(n, me, twin)
    cuts = pieces(shard)
    down = r.down()

    if twinned:
        half, quarter = shard // 2, shard // 4
        mid = pl.multiple_of(half + quarter * group, quarter)
        far = pl.multiple_of(half + quarter * (1 - group), quarter)
        spans = [(0, half), (mid, quarter), (far, quarter)]
    else:
        spans = [(0, shard)]
    rung = spans[:2]

    def gather_copy(step, i):
        start, size = spans[i]
        return remote(
            held.at[step - 1, pl.ds(start, size)], held.at[step, pl.ds(start, size)],
            gat_send.at[step, i], gat_recv.at[step, i], down,
        )

    def gather_sib(step, i):
        start, size = spans[i]
        return remote(
            held.at[step, pl.ds(start, size)], held.at[step, pl.ds(shard + start, size)],
            gsib_send.at[step, i], gsib_recv.at[step, i], r.sibling,
        )

    def gather_twin(step):
        part = held.at[step, pl.ds(*spans[1])]
        return remote(part, part, twin_send.at[step], twin_recv.at[step], twin)

    def from_twin(step):
        start, size = spans[2]
        part = held.at[step, pl.ds(start, size)]
        remote(part, part, twin_send.at[step], twin_recv.at[step], twin).wait_recv()
        gather_sib(step, 2).start()

    def mine(step):
        return r.device(-r.step * step, r.core)

    def theirs(step):
        return r.device(r.step * step, 1 - r.core)

    def columns(owner):
        if not aligned:
            return lhs_ref[owner]
        return normed[:, pl.ds(pl.multiple_of(owner * shard, shard), shard)]

    def add(step):
        for i in range(len(spans)):
            gather_sib(step, i).wait_recv()
        left = [columns(mine(step)), columns(theirs(step))]
        if aligned:
            left = [jnp.concatenate(left, 1)]
        deep = 2 * shard // len(left)
        for j in range(0, width, TILE):
            cols = pl.ds(j, TILE)
            hidden[:, cols] += sum(
                jnp.dot(
                    left[k], held[step, k * deep : (k + 1) * deep, cols],
                    preferred_element_type=jnp.float32,
                )
                for k in range(len(left))
            )

    first.wait()
    for i in range(len(spans)):
        if i < len(rung):
            gather_copy(1, i).start()
        gather_sib(0, i).start()
    head_ref[...] = jnp.zeros_like(head_ref)
    for k in range(3):
        head_ref[16 * k : 16 * k + nact + 1] = weight_ref[...]
    spread(n, me, lambda peer: stat, stats, small_sems.at[4], small_sems.at[5])
    stats[me] = stat[...]

    @pl.loop(0, rows // STRIP)
    def _(t):
        strip = pl.ds(pl.multiple_of(t * STRIP, STRIP), STRIP)
        xf = x_ref[strip].astype(jnp.float32)
        hidden[strip] = xf
        if aligned:
            scale = lax.rsqrt(jnp.mean(xf * xf, -1, keepdims=True) + NORM_EPS)
            normed[strip] = (xf * scale * gain_ref[...]).astype(jnp.bfloat16)

    def gather_hop(step, _):
        for i in range(len(rung)):
            gather_copy(step, i).wait_recv()

            @pl.when(step < last)
            def _():
                gather_copy(step + 1, i).start()

            gather_sib(step, i).start()
            if i == 1:
                gather_twin(step).start()
            elif twinned:
                @pl.when(step > 1)
                def _():
                    from_twin(step - 1)
        add(step - 1)
        return 0

    lax.fori_loop(1, r.ring, gather_hop, 0)
    if twinned:
        from_twin(last)
    add(last)

    @pl.loop(0, rows // STRIP)
    def _(t):
        strip = pl.ds(pl.multiple_of(t * STRIP, STRIP), STRIP)
        h = hidden[strip]
        hidden_b[strip] = h.astype(jnp.bfloat16)
        scale = lax.rsqrt(jnp.mean(h * h, -1, keepdims=True) + NORM_EPS)
        rinv[strip] = scale
        hnorm_b[strip] = (h * scale).astype(jnp.bfloat16)

    slots = n * per
    place = (
        lax.broadcasted_iota(jnp.int32, (slots, rows), 0)
        == jnp.broadcast_to(slot_ref[...], (slots, rows))
    ).astype(jnp.float32).astype(jnp.bfloat16)
    for j in range(0, width, TILE):
        cols = pl.ds(j, TILE)
        moved = jnp.dot(place, hidden_b[:, cols], preferred_element_type=jnp.float32)
        ordered[:, :, cols] = moved.reshape(n, per, TILE).astype(jnp.bfloat16)

    def row_copy(peer):
        return remote(ordered.at[peer], out_ref.at[me], small_sems.at[6], small_sems.at[7], peer)

    @pl.loop(1, burst)
    def _(k):
        row_copy(lax.rem(me + k, n)).start()

    def more_rows(step):
        for u in range(2):
            k = burst + 2 * step + u

            @pl.when(k < n)
            def _():
                row_copy(lax.rem(me + k, n)).start()

    kept = pltpu.make_async_copy(ordered.at[me], out_ref.at[me], local_sem.at[1])
    kept.start()

    collect(n, stats, small_sems.at[5])
    sums = jnp.sum(stats[...], 0)
    total_rows = rows * n
    mean_adv = sums[0:1, 0:1] / total_rows
    var_adv = sums[0:1, 1:2] / total_rows - mean_adv * mean_adv
    advant = ((gae - mean_adv) * lax.rsqrt(var_adv + NORM_EPS)).astype(jnp.bfloat16).astype(jnp.float32)
    returns = adv_ref[1:2].astype(jnp.bfloat16).astype(jnp.float32)
    scale = 1.0 / jnp.sqrt(jnp.full((1, 1), total_rows, jnp.float32))
    heads = lax.dot_general(
        head_ref[0:16], hnorm_b[...], (((1,), (1,)), ((), ())), preferred_element_type=jnp.float32
    )
    square = (nact, nact)
    diagonal = lax.broadcasted_iota(jnp.int32, square, 0) == lax.broadcasted_iota(jnp.int32, square, 1)
    std_dev = jnp.exp(
        jnp.sum(jnp.where(diagonal, jnp.broadcast_to(std_ref[...], square), 0.0), 1, keepdims=True)
    )
    offset = mean_ref[...].astype(jnp.float32) - heads[0:nact]
    sample = noise_ref[...].astype(jnp.float32)
    logr = jnp.sum(
        -sample * offset / std_dev - offset * offset / (2.0 * std_dev * std_dev), 0, keepdims=True
    )
    ratio = jnp.exp(logr)
    clipped = jnp.clip(ratio, 1.0 - CLIP_EPS, 1.0 + CLIP_EPS)
    gratio = jnp.where(ratio * advant <= clipped * advant, -scale * advant, 0.0)
    glogr = gratio * ratio
    ghead[...] = jnp.zeros_like(ghead)
    ghead[0:nact] = glogr * (sample / std_dev + offset / (std_dev * std_dev))
    ghead[nact : nact + 1] = scale * (heads[nact : nact + 1] - returns)
    std_local = jnp.sum(
        glogr * (sample * offset / std_dev + offset * offset / (std_dev * std_dev)), 1, keepdims=True
    )
    rest = ghead[...]
    for k in range(3):
        term = rest.astype(jnp.bfloat16)
        ghead3[16 * k : 16 * k + 16] = term
        rest = rest - term.astype(jnp.float32)

    @pl.loop(0, rows // STRIP)
    def _(t):
        strip = pl.ds(pl.multiple_of(t * STRIP, STRIP), STRIP)
        ghn = lax.dot_general(
            ghead3[:, strip], head_ref[...], (((0,), (0,)), ((), ())),
            preferred_element_type=jnp.float32,
        )
        hnorm = hidden[strip] * rinv[strip]
        inner = jnp.mean(ghn * hnorm, -1, keepdims=True)
        ghid[strip] = (rinv[strip] * (ghn - hnorm * inner)).astype(jnp.bfloat16)

    def product(owner, cols):
        return lax.dot_general(
            columns(owner), ghid[:, cols], (((0,), (0,)), ((), ())),
            preferred_element_type=jnp.float32,
        )

    def ring_copy(step, i):
        return remote(
            ring_out.at[step, cuts[i]], ring_in.at[step, cuts[i]],
            ring_send.at[step, i], ring_recv.at[step, i], down,
        )

    def sib_copy(step):
        return remote(
            sib_out.at[step], sib_in.at[step], sib_send.at[step], sib_recv.at[step], r.sibling
        )

    def terms(step):
        other = r.device(-r.step * (last - step), 1 - r.core)
        for j in range(0, width, TILE):
            cols = pl.ds(j, TILE)
            sib_out[step, :, cols] = product(other, cols).astype(jnp.bfloat16)
        sib_copy(step).start()
        target = r.device(r.step * (last - step), r.core)
        for j in range(0, width, TILE):
            cols = pl.ds(j, TILE)
            own[:, cols] = product(target, cols)
        sib_copy(step).wait_recv()

    terms(0)
    for i, cut in enumerate(cuts):
        ring_out[0, cut] = (own[cut] + sib_in[0, cut].astype(jnp.float32)).astype(jnp.bfloat16)
        ring_copy(0, i).start()
    more_rows(0)

    head_local = jnp.dot(ghead3[...], hnorm_b[...], preferred_element_type=jnp.float32)
    head_local = head_local[0:16] + head_local[16:32] + head_local[32:48]
    share = width // n
    diagonal = lax.broadcasted_iota(jnp.int32, (nact, share), 0) == lax.broadcasted_iota(
        jnp.int32, (nact, share), 1
    )
    std_row = jnp.sum(jnp.where(diagonal, std_local, 0.0), 0, keepdims=True)
    line = lax.broadcasted_iota(jnp.int32, (16, share), 0)
    for j in range(n):
        head_out[j] = jnp.where(
            line == nact + 1, std_row, head_local[:, j * share : (j + 1) * share]
        )
    spread(n, me, lambda peer: head_out.at[peer], head_in, small_sems.at[0], small_sems.at[1])
    head_in[me] = head_out[me]

    def hop(step, _):
        terms(step)
        for i, cut in enumerate(cuts):
            ring_copy(step - 1, i).wait_recv()
            ring_out[step, cut] = (
                own[cut]
                + sib_in[step, cut].astype(jnp.float32)
                + ring_in[step - 1, cut].astype(jnp.float32)
            ).astype(jnp.bfloat16)
            ring_copy(step, i).start()
        more_rows(step)
        return 0

    lax.fori_loop(1, r.ring // 2, hop, 0)
    collect(n, head_in, small_sems.at[1])
    head_sum[...] = jnp.sum(head_in[...], 0)
    head_all[me] = head_sum[...]
    spread(n, me, lambda peer: head_sum, head_all, small_sems.at[2], small_sems.at[3])
    lax.fori_loop(r.ring // 2, last, hop, 0)
    terms(last)
    more_rows(last)
    for i, cut in enumerate(cuts):
        ring_copy(last - 1, i).wait_recv()
        grad_ref[cut] = (
            own[cut]
            + sib_in[last, cut].astype(jnp.float32)
            + ring_in[last - 1, cut].astype(jnp.float32)
        )
    collect(n, head_all, small_sems.at[3])
    for j in range(n):
        heads_ref[:, j * share : (j + 1) * share] = head_all[j]
    kept.wait()
    collect(n, out_ref, small_sems.at[7])
    collect(n, ordered, small_sems.at[6])
    collect(n, stats, small_sems.at[4])
    collect(n, head_in, small_sems.at[0])
    collect(n, head_all, small_sems.at[2])

    def drain(step, _):
        for i in range(len(spans)):
            gather_sib(step, i).wait_send()
        for i in range(len(rung)):
            @pl.when(step < last)
            def _():
                gather_copy(step + 1, i).wait_send()

        for i in range(len(cuts)):
            @pl.when(step < last)
            def _():
                ring_copy(step, i).wait_send()

        if twinned:
            @pl.when(step > 0)
            def _():
                gather_twin(step).wait_send()

        sib_copy(step).wait_send()
        return 0

    lax.fori_loop(0, r.ring, drain, 0)


def step_call(n, groups, x, weight, gain, adv, slot, old_mean, noise, head, log_std):
    rows, width = x.shape
    shard = weight.shape[0]
    nact = log_std.shape[0]
    per = -(-(rows // n) // 8) * 8
    aligned = shard % 128 == 0
    twinned = groups == 2 and shard % 64 == 0
    blocks = []
    if not aligned:
        xf = x.astype(jnp.float32)
        normed = xf * lax.rsqrt(jnp.mean(xf * xf, -1, keepdims=True) + NORM_EPS) * gain
        blocks = [normed.astype(jnp.bfloat16).reshape(rows, n, shard).transpose(1, 0, 2)]
    count = len(pieces(shard))
    ring = n // 2
    share = width // n
    vmem = pl.BlockSpec(memory_space=pltpu.VMEM)
    anywhere = pl.BlockSpec(memory_space=pl.ANY)
    sems = pltpu.SemaphoreType.DMA
    bf16, f32 = jnp.bfloat16, jnp.float32
    fixed = functools.partial(step_kernel, n, nact, per, max(n // 2, 1), aligned, twinned)

    def body(*refs):
        given = 9
        lhs = refs[given] if blocks else None
        fixed(*refs[:given], lhs, *refs[given + len(blocks) :])

    return pl.pallas_call(
        body,
        name="step",
        out_shape=(
            jax.ShapeDtypeStruct((n, per, width), bf16),
            jax.ShapeDtypeStruct((shard, width), f32),
            jax.ShapeDtypeStruct((16, width), f32),
        ),
        in_specs=[vmem, anywhere] + [vmem] * (7 + len(blocks)),
        out_specs=(anywhere, vmem, vmem),
        scratch_shapes=[
            pltpu.VMEM((rows, width) if aligned else (16, 128), bf16),
            pltpu.VMEM((ring, 2 * shard, width), bf16),
            pltpu.VMEM((rows, width), f32),
            pltpu.VMEM((rows, width), bf16),
            pltpu.VMEM((rows, width), bf16),
            pltpu.VMEM((rows, 1), f32),
            pltpu.VMEM((rows, width), bf16),
            pltpu.VMEM((16, rows), f32),
            pltpu.VMEM((48, rows), bf16),
            pltpu.VMEM((n, per, width), bf16),
            pltpu.VMEM((8, 128), f32),
            pltpu.VMEM((n, 8, 128), f32),
            pltpu.VMEM((shard, width), f32),
            pltpu.VMEM((ring, shard, width), bf16),
            pltpu.VMEM((ring, shard, width), bf16),
            pltpu.VMEM((ring - 1, shard, width), bf16),
            pltpu.VMEM((ring - 1, shard, width), bf16),
            pltpu.VMEM((n, 16, share), f32),
            pltpu.VMEM((n, 16, share), f32),
            pltpu.VMEM((16, share), f32),
            pltpu.VMEM((n, 16, share), f32),
            sems((2,)),
            sems((ring, 2 if twinned else 1)),
            sems((ring, 2 if twinned else 1)),
            sems((ring, 3 if twinned else 1)),
            sems((ring, 3 if twinned else 1)),
            sems((ring if twinned else 1,)),
            sems((ring if twinned else 1,)),
            pltpu.VMEM((48, width), bf16),
            sems((ring - 1, count)),
            sems((ring - 1, count)),
            sems((ring,)),
            sems((ring,)),
            sems((8,)),
        ],
        compiler_params=pltpu.CompilerParams(
            collective_id=0, has_side_effects=True, vmem_limit_bytes=66_000_000
        ),
        cost_estimate=pl.CostEstimate(
            flops=4 * rows * width * width, bytes_accessed=32 * rows * width, transcendentals=0
        ),
    )(x, weight, gain[None], adv, slot, old_mean, noise, head, log_std[None], *blocks)


def advantages(reward, value_old, done):
    keep = 1.0 - done.astype(jnp.float32)
    deltas = reward + GAMMA * value_old[:, 1:] * keep - value_old[:, :-1]

    carry = jnp.zeros((reward.shape[0],), jnp.float32)
    column = []
    for t in reversed(range(reward.shape[1])):
        carry = deltas[:, t] + GAMMA * LAMBDA_GAE * keep[:, t] * carry
        column.append(carry)
    gae = jnp.stack(column[::-1], 1)
    return (gae.reshape(-1), (gae + value_old[:, :-1]).reshape(-1))


def local(
    obs_feat,
    reward,
    value_old,
    done,
    minibatch_perm,
    old_mean,
    noise,
    gain_in,
    out_weight,
    head_weight,
    log_std,
):
    gae, returns = advantages(reward, value_old, done)
    local_rows, width = obs_feat.shape
    devices = lax.axis_size("fsdp")
    nact = log_std.shape[0]
    per_peer = local_rows // devices
    padded = -(-per_peer // 8) * 8
    slot = minibatch_perm // local_rows * padded + minibatch_perm % per_peer
    moved, grad_weight, heads_all = step_call(
        devices, lax.axis_size("groups"), obs_feat, out_weight, gain_in, jnp.stack([gae, returns]),
        slot[None], old_mean.T, noise.T, head_weight.T, log_std,
    )
    hidden_out = moved[:, :per_peer].reshape(local_rows, width)
    grad_head = heads_all[: nact + 1].T
    grad_std = heads_all[nact + 1, :nact]
    return (hidden_out, grad_weight, grad_head, grad_std)


def solution(mesh):
    return jax.shard_map(
        local,
        mesh=mesh,
        in_specs=(
            P(("groups", "fsdp"), None),
            P(("groups", "fsdp"), None),
            P(("groups", "fsdp"), None),
            P(("groups", "fsdp"), None),
            P(("groups", "fsdp")),
            P(("groups", "fsdp"), None),
            P(("groups", "fsdp"), None),
            P(),
            P("fsdp", None),
            P(),
            P(),
        ),
        out_specs=(
            P(("groups", "fsdp"), None),
            P(("groups", "fsdp"), None),
            P("groups", None),
            P("groups"),
        ),
        check_vma=False,
    )
```
